32 devices in a mesh: level: 2 (over y), sub: 16 (over z, x, core).
Axes of the slice: x: 2, y: 2, z: 4, core: 2. Of those that a mesh axis runs over, the one named last changes fastest.
Arguments:
- factor_inv: float32 [2, 16, 256, 256], P('level', 'sub'), may hold values from -0.0625 to 1.4, as said below
- update_blocks: float32 [2, 16, 4, 128, 256], P('level', 'sub'), may hold values from -0.1875 to 0.1875
- update_rows: int32 [2, 16, 4], P('level', 'sub'), may hold values from 0 to 3, each once within a row
- right_side: float32 [2, 16, 256, 512], P('level', 'sub'), may hold values from -4000 to 4000
Outputs:
- solution: float32 [2, 16, 256, 512], P('level', 'sub')
The draws below stay inside these ranges and needn't reach their ends.
Inputs may be any that keep to these rules, and one draw needn't show every extreme that they name: `update_rows`: each supernode's 4 update blocks name the 4 target row blocks once each; values below 2 are row blocks of the parent supernode in the same subtree, the others those of the parent supernode in the next subtree (the last subtree's next is the first). `factor_inv`: each 256 x 256 block is lower triangular, with diagonal entries between 0.7 and 1.4.
All inputs are finite; a program needn't handle non-finite values.
Results may differ from the reference program's by a relative error of at most 0.00014.
Values sent between devices are 32-bit elements; how exact they have to be, the bound alone decides.
A program may use at most 64 MiB of HBM per device.

```python
import math
import jax
import jax.numpy as jnp
from jax import lax

W = 256
BLK = 128
R = 512
NRB = 2
K = 4
N_LEVEL = 2
N_SUB = 16


def draw_factor_inv(key, part):
    full_shape = (N_LEVEL, N_SUB, W, W)
    key_one, key_two = jax.random.split(key, 2)
    row_index = lax.broadcasted_iota(jnp.int32, full_shape, 2)
    col_index = lax.broadcasted_iota(jnp.int32, full_shape, 3)
    off_diag = jnp.clip(0.6 * jax.random.normal(key_one, full_shape, jnp.float32), -1.0, 1.0)
    diag_vals = jnp.exp(jax.random.uniform(key_two, full_shape, jnp.float32, math.log(0.7), math.log(1.4)))
    off_diag = off_diag / math.sqrt(W)
    return jnp.where(row_index > col_index, off_diag, jnp.where(row_index == col_index, diag_vals, 0.0)).astype(jnp.float32)


def draw_right_side(key, part):
    full_shape = (N_LEVEL, N_SUB, W, R)
    key_one, key_two, key_three = jax.random.split(key, 3)
    position = (lax.broadcasted_iota(jnp.float32, full_shape, 0) * N_SUB + lax.broadcasted_iota(jnp.float32, full_shape, 1)) / max(N_LEVEL * N_SUB - 1, 1)
    rise_factor = 1.0 + 2.0 * position
    row_scale = jnp.exp(jax.random.uniform(key_two, (N_LEVEL, N_SUB, W, 1), jnp.float32, 0.0, math.log(10.0)))
    col_scale = jnp.exp(jax.random.uniform(key_three, (1, 1, 1, R), jnp.float32, 0.0, math.log(10.0)))
    base_vals = jnp.clip(jax.random.normal(key_one, full_shape, jnp.float32), -4.0, 4.0)
    return (base_vals * rise_factor * row_scale * col_scale).astype(jnp.float32)


def shard_levels(stream_key, extent, shards, low, top_value):
    level, own = 1.0, jax.random.fold_in(stream_key, 6)
    for dim, parts in shards:
        draws = jnp.exp(jax.random.uniform(jax.random.fold_in(own, dim), (parts,), jnp.float32, low / len(shards), top_value / len(shards)))
        level = level * jnp.repeat(draws, extent[dim] // parts).reshape([-1 if axis == dim else 1 for axis in range(len(extent))])
    return level


def noise(rng, extent, width, most, cuts=(), held_as=jnp.bfloat16):
    array = jax.random.normal(rng, extent, jnp.float32) * width
    if len(cuts) > 0:
        array = shard_levels(rng, extent, cuts, -0.22, 0.18) * array
    return jnp.clip(array, min=-most, max=most).astype(held_as)


def setup_inputs(seed: int = 0) -> dict:
    keys = jax.random.split(jax.random.key(seed), 5)
    return {
        "factor_inv": draw_factor_inv(jax.random.fold_in(keys[4], 71), 0),
        "update_blocks": noise(keys[1], (N_LEVEL, N_SUB, K, BLK, W), (4 * W) ** -0.5, 0.1875, ((0, 2), (1, 16)), jnp.float32),
        "update_rows": jax.vmap(lambda own: jax.random.permutation(own, K))(jax.random.split(keys[2], N_LEVEL * N_SUB)).reshape((N_LEVEL, N_SUB, K)).astype(jnp.int32),
        "right_side": draw_right_side(jax.random.fold_in(keys[4], 71), 0),
    }


FULL_PRECISION = lax.Precision.HIGHEST

def reference(factor_inv, update_blocks, update_rows, right_side):
    norm_total = lax.optimization_barrier(jnp.sum(right_side * right_side, axis=(0, 1, 2)))
    col_scale = jnp.sqrt(norm_total / (N_LEVEL * N_SUB * W) + 1e-06)
    onehot = (update_rows[:, :, :, None] == jnp.arange(K, dtype=jnp.int32)[None, None, None, :]).astype(jnp.float32)
    incoming = jnp.zeros((N_SUB, W, R), jnp.float32)
    forward = []
    for level_no in range(N_LEVEL):
        forward_val = jnp.einsum('sij,sjc->sic', factor_inv[level_no], right_side[level_no] - incoming, precision=FULL_PRECISION)
        forward.append(forward_val)
        if level_no + 1 < N_LEVEL:
            pieces = jnp.einsum('skbj,sjc->skbc', update_blocks[level_no], forward_val, precision=FULL_PRECISION)
            slot_sums = jnp.einsum('skd,skbc->sdbc', onehot[level_no], pieces, precision=FULL_PRECISION)
            incoming = (slot_sums[:, :NRB] + jnp.roll(slot_sums[:, NRB:], 1, axis=0)).reshape(N_SUB, W, R)
    result_levels = [forward[0]] * N_LEVEL
    parent_x = jnp.zeros((N_SUB, W, R), jnp.float32)
    for level_no in reversed(range(N_LEVEL)):
        rhs_now = forward[level_no]
        if level_no + 1 < N_LEVEL:
            own_blocks = parent_x.reshape(N_SUB, NRB, BLK, R)
            paired = jnp.concatenate([own_blocks, jnp.roll(own_blocks, -1, axis=0)], axis=1)
            picked = jnp.einsum('skd,sdbc->skbc', onehot[level_no], paired, precision=FULL_PRECISION)
            rhs_now = rhs_now - jnp.einsum('skbj,skbc->sjc', update_blocks[level_no], picked, precision=FULL_PRECISION)
        parent_x = jnp.einsum('sji,sjc->sic', factor_inv[level_no], rhs_now, precision=FULL_PRECISION)
        result_levels[level_no] = parent_x
    return jnp.stack(result_levels) / col_scale
```

```python
import functools

import jax
import jax.numpy as jnp
from jax import lax
from jax.experimental import pallas as pl
from jax.experimental.pallas import tpu as pltpu
from jax.sharding import PartitionSpec as P

LANES = 128
MESH = pl.DeviceIdType.MESH


def halves(value):
    high = value.astype(jnp.bfloat16)
    low = (value - high.astype(jnp.float32)).astype(jnp.bfloat16)
    return high, low


def left_operand(matrix):
    high, low = halves(matrix)
    return jnp.concatenate([high, low, high], axis=1)


def right_operand(values):
    high, low = halves(values)
    return jnp.concatenate([high, high, low], axis=0)


def product(left, right):
    return jnp.dot(left, right, preferred_element_type=jnp.float32)


def flipped(index, bit):
    return index + bit - 2 * bit * lax.rem(lax.div(index, bit), 2)


def kernel(
    levels,
    subs,
    rows_ref,
    inverse_hbm,
    blocks_hbm,
    rhs_hbm,
    x_ref,
    total_ref,
    inverse,
    blocks,
    rhs,
    spread_own,
    spread_next,
    turned_own,
    turned_next,
    gram,
    base,
    next_out,
    next_in,
    up_out,
    up_in,
    own_in,
    beside_in,
    solved,
    sums_out,
    sums_in,
    load_sem,
    next_send,
    next_recv,
    up_send,
    up_recv,
    down_send,
    down_recv,
    side_send,
    side_recv,
    sums_send,
    sums_recv,
):
    level = lax.axis_index("level")
    sub = lax.axis_index("sub")
    chunks = rhs.shape[0]
    width = inverse.shape[0]
    slots = blocks.shape[0]
    right = lax.rem(sub + 1, subs)
    left = lax.rem(sub + subs - 1, subs)
    has_up = level < levels - 1
    has_down = level > 0
    above = {"level": level + 1}
    below = {"level": level - 1}

    loads = [
        pltpu.make_async_copy(blocks_hbm, blocks, load_sem.at[0]),
        pltpu.make_async_copy(inverse_hbm, inverse, load_sem.at[1]),
    ]
    for c in range(chunks):
        loads.append(
            pltpu.make_async_copy(
                rhs_hbm.at[:, pl.ds(c * LANES, LANES)], rhs.at[c], load_sem.at[2 + c]
            )
        )
    for load in loads:
        load.start()

    partners = []
    bit = 1
    while bit < subs:
        partners.append({"sub": flipped(sub, bit)})
        bit *= 2
    assert bit == subs
    sub_rounds = len(partners)
    bit = 1
    while bit < levels:
        partners.append({"level": flipped(level, bit)})
        bit *= 2
    assert bit == levels
    rounds = len(partners)

    barrier = pltpu.get_barrier_semaphore()
    for partner in partners:
        pl.semaphore_signal(barrier, inc=1, device_id=partner, device_id_type=MESH)

    @pl.when(has_up)
    def _():
        for partner in (above, {"sub": right}, {"sub": left}):
            pl.semaphore_signal(barrier, inc=1, device_id=partner, device_id_type=MESH)

    @pl.when(has_down)
    def _():
        pl.semaphore_signal(barrier, inc=1, device_id=below, device_id_type=MESH)

    def remote(source, target, send, recv, device):
        return pltpu.make_async_remote_copy(
            src_ref=source,
            dst_ref=target,
            send_sem=send,
            recv_sem=recv,
            device_id=device,
            device_id_type=MESH,
        )

    next_copy = [
        remote(next_out.at[c], next_in.at[c], next_send.at[c], next_recv.at[c], {"sub": right})
        for c in range(chunks)
    ]
    up_copy = [
        remote(up_out.at[c], up_in.at[c], up_send.at[c], up_recv.at[c], above)
        for c in range(chunks)
    ]
    down_copy = [
        remote(solved.at[c], own_in.at[c], down_send.at[c], down_recv.at[c], below)
        for c in range(chunks)
    ]
    side_copy = [
        remote(own_in.at[c], beside_in.at[c], side_send.at[c], side_recv.at[c], {"sub": left})
        for c in range(chunks)
    ]
    sums_copy = [
        remote(sums_out.at[r], sums_in.at[r], sums_send.at[r], sums_recv.at[r], partners[r])
        for r in range(rounds)
    ]

    loads[0].wait()
    loads[1].wait()

    def placed(slot):
        found = jnp.int32(0)
        for k in range(slots):
            found = jnp.where(rows_ref[k] == slot, k, found)
        return blocks[found]

    def spread_matrix(first):
        picked = [placed(first + d) for d in range(slots // 2)]
        ordered = jnp.concatenate(picked, axis=0)
        return product(left_operand(ordered), right_operand(inverse[...]))

    def make_next():
        matrix = spread_matrix(slots // 2)
        spread_next[...] = left_operand(matrix)
        turned_next[...] = left_operand(matrix.T)

    def make_own():
        matrix = spread_matrix(0)
        spread_own[...] = left_operand(matrix)
        turned_own[...] = left_operand(matrix.T)

    def make_gram():
        gram[...] = product(left_operand(inverse[...].T), right_operand(inverse[...]))

    def make_base(operand, c):
        base[c] = product(left_operand(gram[...]), operand)

    @pl.when(has_up)
    def _():
        make_next()

    for load in loads[2:]:
        load.wait()

    greetings = rounds + jnp.where(has_up, 3, 0) + jnp.where(has_down, 1, 0)
    pl.semaphore_wait(barrier, greetings)

    def start_sums():
        for c in range(chunks):
            value = rhs[c]
            squares = (value * value).reshape(width // 8, 8, LANES)
            sums_out[0, :, pl.ds(c * LANES, LANES)] = jnp.sum(squares, axis=0)
        sums_copy[0].start()

    def next_sums(r):
        if r >= rounds:
            return
        sums_copy[r - 1].wait_recv()
        sums_out[r] = sums_out[r - 1] + sums_in[r - 1]
        sums_copy[r].start()

    def send_next(operand, c):
        next_out[c] = product(spread_next[...], operand)
        next_copy[c].start()

    def send_up(operand, c):
        value = product(spread_own[...], operand)
        next_copy[c].wait_recv()
        up_out[c] = value + next_in[c]
        up_copy[c].start()

    @pl.when(level == 0)
    def _():
        for c in range(chunks):
            send_next(right_operand(rhs[c]), c)
        make_own()
        start_sums()
        for c in range(chunks):
            send_up(right_operand(rhs[c]), c)
            if c + 1 < sub_rounds:
                next_sums(c + 1)
        make_gram()
        for r in range(chunks + 1, sub_rounds):
            next_sums(r)
        for c in range(chunks):
            make_base(right_operand(rhs[c]), c)
        next_sums(sub_rounds)

    @pl.when(has_down)
    def _():
        start_sums()
        make_gram()

        @pl.when(has_up)
        def _():
            make_own()

        for r in range(1, sub_rounds + 1):
            next_sums(r)
        for c in range(chunks):
            up_copy[c].wait_recv()
            operand = right_operand(rhs[c] - up_in[c])

            @pl.when(has_up)
            def _():
                send_next(operand, c)
                send_up(operand, c)

            make_base(operand, c)

            @pl.when(jnp.logical_not(has_up))
            def _():
                value = base[c]
                solved[c] = value
                down_copy[c].start()
                x_ref[:, pl.ds(c * LANES, LANES)] = value

    @pl.when(has_up)
    def _():
        for c in range(chunks):
            down_copy[c].wait_recv()
            side_copy[c].start()
            value = base[c] - product(turned_own[...], right_operand(own_in[c]))
            side_copy[c].wait_recv()
            value = value - product(turned_next[...], right_operand(beside_in[c]))
            x_ref[:, pl.ds(c * LANES, LANES)] = value

            @pl.when(has_down)
            def _():
                solved[c] = value
                down_copy[c].start()

    for r in range(sub_rounds + 1, rounds):
        next_sums(r)
    sums_copy[rounds - 1].wait_recv()
    total_ref[...] = sums_out[rounds - 1] + sums_in[rounds - 1]

    for r in range(rounds):
        sums_copy[r].wait_send()

    @pl.when(has_up)
    def _():
        for c in range(chunks):
            next_copy[c].wait_send()
            up_copy[c].wait_send()
            side_copy[c].wait_send()

    @pl.when(has_down)
    def _():
        for c in range(chunks):
            down_copy[c].wait_send()


def per_device(factor_inv, update_blocks, update_rows, right_side):
    levels = lax.axis_size("level")
    subs = lax.axis_size("sub")
    width = factor_inv.shape[-1]
    columns = right_side.shape[-1]
    slots, block_rows = update_blocks.shape[2:4]
    chunks = columns // LANES
    rounds = (levels * subs).bit_length() - 1
    piece = pltpu.VMEM((chunks, width, LANES), jnp.float32)
    wide = pltpu.VMEM((width, 3 * width), jnp.bfloat16)
    chunk_sem = pltpu.SemaphoreType.DMA((chunks,))
    round_sem = pltpu.SemaphoreType.DMA((rounds,))
    any_space = pl.BlockSpec(memory_space=pl.ANY)
    in_vmem = pl.BlockSpec(memory_space=pltpu.VMEM)
    value, total = pl.pallas_call(
        functools.partial(kernel, levels, subs),
        out_shape=[
            jax.ShapeDtypeStruct((width, columns), jnp.float32),
            jax.ShapeDtypeStruct((8, columns), jnp.float32),
        ],
        in_specs=[
            pl.BlockSpec(memory_space=pltpu.SMEM),
            any_space,
            any_space,
            any_space,
        ],
        out_specs=[in_vmem, in_vmem],
        scratch_shapes=[
            pltpu.VMEM((width, width), jnp.float32),
            pltpu.VMEM((slots, block_rows, width), jnp.float32),
            piece,
            wide,
            wide,
            wide,
            wide,
            pltpu.VMEM((width, width), jnp.float32),
            piece,
            piece,
            piece,
            piece,
            piece,
            piece,
            piece,
            piece,
            pltpu.VMEM((rounds, 8, columns), jnp.float32),
            pltpu.VMEM((rounds, 8, columns), jnp.float32),
            pltpu.SemaphoreType.DMA((2 + chunks,)),
        ]
        + [chunk_sem] * 8
        + [round_sem] * 2,
        compiler_params=pltpu.CompilerParams(
            collective_id=0, has_side_effects=True, vmem_limit_bytes=40 * 1024 * 1024
        ),
        name="staircase",
    )(update_rows[0, 0], factor_inv[0, 0], update_blocks[0, 0], right_side[0, 0])
    norm_total = jnp.sum(total, axis=0)
    col_scale = jnp.sqrt(norm_total / (levels * subs * width) + 1e-06)
    return (value / col_scale)[None, None]


def solution(mesh):
    return jax.shard_map(
        per_device,
        mesh=mesh,
        in_specs=(
            P("level", "sub", None, None),
            P("level", "sub", None, None, None),
            P("level", "sub", None),
            P("level", "sub", None, None),
        ),
        out_specs=P("level", "sub", None, None),
        check_vma=False,
    )
```

```python
import functools

import jax
import jax.numpy as jnp
from jax import lax
from jax.experimental import pallas as pl
from jax.experimental.pallas import tpu as pltpu
from jax.sharding import PartitionSpec as P

LANES = 128
MESH = pl.DeviceIdType.MESH


def halves(value):
    high = value.astype(jnp.bfloat16)
    low = (value - high.astype(jnp.float32)).astype(jnp.bfloat16)
    return high, low


def left_operand(matrix):
    high, low = halves(matrix)
    return jnp.concatenate([high, low, high], axis=1)


def right_operand(values):
    high, low = halves(values)
    return jnp.concatenate([high, high, low], axis=0)


def product(left, right):
    return jnp.dot(left, right, preferred_element_type=jnp.float32)


def flipped(index, bit):
    return index + bit - 2 * bit * lax.rem(lax.div(index, bit), 2)


def kernel(
    levels,
    subs,
    rows_ref,
    inverse_hbm,
    blocks_hbm,
    rhs_hbm,
    x_ref,
    total_ref,
    inverse,
    blocks,
    rhs,
    spread_own,
    spread_next,
    turned_own,
    turned_next,
    gram,
    gram_top,
    base,
    own,
    next_out,
    next_in,
    up_in,
    own_in,
    beside_in,
    solved,
    top_corner,
    top_rows,
    top_rhs,
    sums_out,
    sums_in,
    load_sem,
    give_send,
    give_recv,
    next_send,
    next_recv,
    up_send,
    up_recv,
    down_send,
    down_recv,
    side_send,
    side_recv,
    sums_send,
    sums_recv,
):
    level = lax.axis_index("level")
    sub = lax.axis_index("sub")
    chunks = rhs.shape[0]
    width = inverse.shape[0]
    half = width // 2
    slots = blocks.shape[0]
    right = lax.rem(sub + 1, subs)
    left = lax.rem(sub + subs - 1, subs)
    is_top = level == levels - 1
    is_host = level == levels - 2
    has_up = level < levels - 1
    above = {"level": level + 1}
    below = {"level": level - 1}

    block_load = pltpu.make_async_copy(blocks_hbm, blocks, load_sem.at[0])
    inverse_load = pltpu.make_async_copy(inverse_hbm, inverse, load_sem.at[1])
    rhs_loads = [
        pltpu.make_async_copy(
            rhs_hbm.at[:, pl.ds(c * LANES, LANES)], rhs.at[c], load_sem.at[2 + c]
        )
        for c in range(chunks)
    ]

    @pl.when(has_up)
    def _():
        block_load.start()
        inverse_load.start()

    for load in rhs_loads:
        load.start()

    partners = []
    bit = 1
    while bit < subs:
        partners.append({"sub": flipped(sub, bit)})
        bit *= 2
    assert bit == subs
    sub_rounds = len(partners)
    bit = 1
    while bit < levels:
        partners.append({"level": flipped(level, bit)})
        bit *= 2
    assert bit == levels
    rounds = len(partners)

    barrier = pltpu.get_barrier_semaphore()
    for partner in partners:
        pl.semaphore_signal(barrier, inc=1, device_id=partner, device_id_type=MESH)

    @pl.when(has_up)
    def _():
        for partner in (above, {"sub": right}, {"sub": left}):
            pl.semaphore_signal(barrier, inc=1, device_id=partner, device_id_type=MESH)

    @pl.when(level > 0)
    def _():
        pl.semaphore_signal(barrier, inc=1, device_id=below, device_id_type=MESH)

    def remote(source, target, send, recv, device):
        return pltpu.make_async_remote_copy(
            src_ref=source,
            dst_ref=target,
            send_sem=send,
            recv_sem=recv,
            device_id=device,
            device_id_type=MESH,
        )

    def chunk_copies(source, target, send, recv, device):
        return [
            remote(source.at[c], target.at[c], send.at[c], recv.at[c], device)
            for c in range(chunks)
        ]

    give_copy = [
        remote(
            inverse_hbm.at[pl.ds(0, half), pl.ds(0, half)],
            top_corner,
            give_send.at[0],
            give_recv.at[0],
            below,
        ),
        remote(
            inverse_hbm.at[pl.ds(half, half)], top_rows, give_send.at[1], give_recv.at[1], below
        ),
    ]
    for c in range(chunks):
        give_copy.append(
            remote(
                rhs_hbm.at[:, pl.ds(c * LANES, LANES)],
                top_rhs.at[c],
                give_send.at[2 + c],
                give_recv.at[2 + c],
                below,
            )
        )
    next_copy = chunk_copies(next_out, next_in, next_send, next_recv, {"sub": right})
    up_copy = chunk_copies(own, up_in, up_send, up_recv, above)
    lift_copy = chunk_copies(own_in, solved, up_send, up_recv, above)
    down_copy = chunk_copies(solved, own_in, down_send, down_recv, below)
    side_copy = chunk_copies(own_in, beside_in, side_send, side_recv, {"sub": left})
    sums_copy = [
        remote(sums_out.at[r], sums_in.at[r], sums_send.at[r], sums_recv.at[r], partners[r])
        for r in range(rounds)
    ]

    def placed(slot):
        found = jnp.int32(0)
        for k in range(slots):
            found = jnp.where(rows_ref[k] == slot, k, found)
        return blocks[found]

    def spread_matrix(first):
        picked = [placed(first + d) for d in range(slots // 2)]
        ordered = jnp.concatenate(picked, axis=0)
        return product(left_operand(ordered), right_operand(inverse[...]))

    def squared(matrix):
        return left_operand(product(left_operand(matrix.T), right_operand(matrix)))

    def start_sums():
        for c in range(chunks):
            value = rhs[c]
            squares = (value * value).reshape(width // 8, 8, LANES)
            sums_out[0, :, pl.ds(c * LANES, LANES)] = jnp.sum(squares, axis=0)
        sums_copy[0].start()

    def next_sums(r):
        if r < rounds:
            sums_copy[r - 1].wait_recv()
            sums_out[r] = sums_out[r - 1] + sums_in[r - 1]
            sums_copy[r].start()

    def store(c, value):
        x_ref[:, pl.ds(c * LANES, LANES)] = value

    greetings = rounds + jnp.where(has_up, 3, 0) + jnp.where(level > 0, 1, 0)

    @pl.when(is_top)
    def _():
        pl.semaphore_wait(barrier, greetings)
        for copy in give_copy:
            copy.start()
        for load in rhs_loads:
            load.wait()
        start_sums()
        for r in range(1, sub_rounds + 1):
            next_sums(r)
        for c in range(chunks):
            lift_copy[c].wait_recv()
            store(c, solved[c])
        for copy in give_copy:
            copy.wait_send()

    def make_next():
        matrix = spread_matrix(slots // 2)
        spread_next[...] = left_operand(matrix)

    def make_own():
        matrix = spread_matrix(0)
        spread_own[...] = left_operand(matrix)

    def make_turned():
        for matrix, turned in ((spread_own, turned_own), (spread_next, turned_next)):
            for piece in range(3):
                span = pl.ds(piece * width, width)
                turned[:, span] = matrix[:, span].T

    def send_next(operand, c):
        next_out[c] = product(spread_next[...], operand)
        next_copy[c].start()

    def finish(c):
        side_copy[c].wait_recv()
        value = base[c] - product(turned_next[...], right_operand(beside_in[c]))
        store(c, value)
        if levels > 2:

            @pl.when(level > 0)
            def _():
                solved[c] = value
                down_copy[c].start()

    @pl.when(has_up)
    def _():
        block_load.wait()
        inverse_load.wait()
        make_next()
        for load in rhs_loads:
            load.wait()
        pl.semaphore_wait(barrier, greetings)

    @pl.when(is_host)
    def _():
        if levels > 2:

            @pl.when(level > 0)
            def _():
                for c in range(chunks):
                    up_copy[c].wait_recv()

        def remaining(c):
            if levels == 2:
                return rhs[c]
            return rhs[c] - jnp.where(level > 0, up_in[c], 0.0)

        for c in range(chunks):
            send_next(right_operand(remaining(c)), c)
        start_sums()
        make_own()
        next_sums(1)
        gram[...] = squared(inverse[...])
        for c in range(chunks):
            operand = right_operand(remaining(c))
            own[c] = product(spread_own[...], operand)
            base[c] = product(gram[...], operand)
            if c + 2 < sub_rounds:
                next_sums(c + 2)
        for r in range(chunks + 2, sub_rounds):
            next_sums(r)
        make_turned()
        give_copy[0].wait_recv()
        give_copy[1].wait_recv()
        corner = jnp.concatenate([top_corner[...], jnp.zeros((half, half), jnp.float32)], axis=1)
        gram_top[...] = squared(jnp.concatenate([corner, top_rows[...]], axis=0))
        for c in range(chunks):
            next_copy[c].wait_recv()
            give_copy[2 + c].wait_recv()
            operand = right_operand(top_rhs[c] - (own[c] + next_in[c]))
            value = product(gram_top[...], operand)
            own_in[c] = value
            side_copy[c].start()
            lift_copy[c].start()
            base[c] = base[c] - product(turned_own[...], right_operand(value))
            if c == 0:
                next_sums(sub_rounds)
            if c > 0:
                finish(c - 1)
        finish(chunks - 1)
        for c in range(chunks):
            next_copy[c].wait_send()
            lift_copy[c].wait_send()
            side_copy[c].wait_send()

    if levels > 2:

        @pl.when(level < levels - 2)
        def _():
            make_own()
            make_turned()
            gram[...] = squared(inverse[...])
            start_sums()
            for r in range(1, sub_rounds + 1):
                next_sums(r)

            @pl.when(level > 0)
            def _():
                for c in range(chunks):
                    up_copy[c].wait_recv()

            for c in range(chunks):
                operand = right_operand(rhs[c] - jnp.where(level > 0, up_in[c], 0.0))
                send_next(operand, c)
                value = product(spread_own[...], operand)
                next_copy[c].wait_recv()
                own[c] = value + next_in[c]
                up_copy[c].start()
                base[c] = product(gram[...], operand)
            for c in range(chunks):
                down_copy[c].wait_recv()
                side_copy[c].start()
                base[c] = base[c] - product(turned_own[...], right_operand(own_in[c]))
                finish(c)
            for c in range(chunks):
                next_copy[c].wait_send()
                up_copy[c].wait_send()
                side_copy[c].wait_send()

        @pl.when(jnp.logical_and(level > 0, has_up))
        def _():
            for c in range(chunks):
                down_copy[c].wait_send()

    for r in range(sub_rounds + 1, rounds):
        next_sums(r)
    sums_copy[rounds - 1].wait_recv()
    total_ref[...] = sums_out[rounds - 1] + sums_in[rounds - 1]
    for r in range(rounds):
        sums_copy[r].wait_send()


def per_device(factor_inv, update_blocks, update_rows, right_side):
    levels = lax.axis_size("level")
    subs = lax.axis_size("sub")
    width = factor_inv.shape[-1]
    columns = right_side.shape[-1]
    slots, block_rows = update_blocks.shape[2:4]
    chunks = columns // LANES
    rounds = (levels * subs).bit_length() - 1
    piece = pltpu.VMEM((chunks, width, LANES), jnp.float32)
    wide = pltpu.VMEM((width, 3 * width), jnp.bfloat16)
    chunk_sem = pltpu.SemaphoreType.DMA((chunks,))
    round_sem = pltpu.SemaphoreType.DMA((rounds,))
    any_space = pl.BlockSpec(memory_space=pltpu.HBM)
    in_vmem = pl.BlockSpec(memory_space=pltpu.VMEM)
    value, total = pl.pallas_call(
        functools.partial(kernel, levels, subs),
        out_shape=[
            jax.ShapeDtypeStruct((width, columns), jnp.float32),
            jax.ShapeDtypeStruct((8, columns), jnp.float32),
        ],
        in_specs=[
            pl.BlockSpec(memory_space=pltpu.SMEM),
            any_space,
            any_space,
            any_space,
        ],
        out_specs=[in_vmem, in_vmem],
        scratch_shapes=[
            pltpu.VMEM((width, width), jnp.float32),
            pltpu.VMEM((slots, block_rows, width), jnp.float32),
            piece,
        ]
        + [wide] * 6
        + [piece] * 8
        + [
            pltpu.VMEM((width // 2, width // 2), jnp.float32),
            pltpu.VMEM((width // 2, width), jnp.float32),
            piece,
            pltpu.VMEM((rounds, 8, columns), jnp.float32),
            pltpu.VMEM((rounds, 8, columns), jnp.float32),
        ]
        + [pltpu.SemaphoreType.DMA((2 + chunks,))] * 3
        + [chunk_sem] * 8
        + [round_sem] * 2,
        compiler_params=pltpu.CompilerParams(
            collective_id=0, has_side_effects=True, vmem_limit_bytes=60 * 1024 * 1024
        ),
        name="staircase",
    )(update_rows[0, 0], factor_inv[0, 0], update_blocks[0, 0], right_side[0, 0])
    norm_total = jnp.sum(total, axis=0)
    col_scale = jnp.sqrt(norm_total / (levels * subs * width) + 1e-06)
    return (value / col_scale)[None, None]


def solution(mesh):
    return jax.shard_map(
        per_device,
        mesh=mesh,
        in_specs=(
            P("level", "sub", None, None),
            P("level", "sub", None, None, None),
            P("level", "sub", None),
            P("level", "sub", None, None),
        ),
        out_specs=P("level", "sub", None, None),
        check_vma=False,
    )
```

```python
import functools

import jax
import jax.numpy as jnp
from jax import lax
from jax.experimental import pallas as pl
from jax.experimental.pallas import tpu as pltpu
from jax.sharding import PartitionSpec as P

LANES = 128
MESH = pl.DeviceIdType.MESH


def halves(value):
    high = value.astype(jnp.bfloat16)
    low = (value - high.astype(jnp.float32)).astype(jnp.bfloat16)
    return high, low


def left_operand(matrix):
    high, low = halves(matrix)
    return jnp.concatenate([high, low, high], axis=1)


def right_operand(values):
    high, low = halves(values)
    return jnp.concatenate([high, high, low], axis=0)


def product(left, right):
    return jnp.dot(left, right, preferred_element_type=jnp.float32)


def flipped(index, bit):
    return index + bit - 2 * bit * lax.rem(lax.div(index, bit), 2)


def kernel(
    levels,
    subs,
    rows_ref,
    inverse_hbm,
    blocks_hbm,
    rhs_hbm,
    x_ref,
    scale_ref,
    inverse,
    blocks,
    rhs,
    spread_own,
    spread_next,
    turned_own,
    turned_next,
    gram,
    gram_top,
    base,
    own,
    next_out,
    next_in,
    up_in,
    own_in,
    beside_in,
    solved,
    top_corner,
    top_rows,
    top_rhs,
    sums_out,
    sums_in,
    load_sem,
    give_send,
    give_recv,
    next_send,
    next_recv,
    up_send,
    up_recv,
    down_send,
    down_recv,
    side_send,
    side_recv,
    sums_send,
    sums_recv,
):
    level = lax.axis_index("level")
    sub = lax.axis_index("sub")
    chunks = rhs.shape[0]
    width = inverse.shape[0]
    half = width // 2
    slots = blocks.shape[0]
    right = lax.rem(sub + 1, subs)
    left = lax.rem(sub + subs - 1, subs)
    is_top = level == levels - 1
    lent = lax.rem(sub, 2) == 0
    is_host = jnp.logical_and(level == levels - 2, lent)
    has_up = level < levels - 1
    above = {"level": level + 1}
    below = {"level": level - 1}

    block_load = pltpu.make_async_copy(blocks_hbm, blocks, load_sem.at[0])
    inverse_load = pltpu.make_async_copy(inverse_hbm, inverse, load_sem.at[1])
    rhs_loads = [
        pltpu.make_async_copy(
            rhs_hbm.at[:, pl.ds(c * LANES, LANES)], rhs.at[c], load_sem.at[2 + c]
        )
        for c in range(chunks)
    ]

    @pl.when(has_up)
    def _():
        block_load.start()

    inverse_load.start()
    for load in rhs_loads:
        load.start()

    partners = []
    bit = 1
    while bit < subs:
        partners.append({"sub": flipped(sub, bit)})
        bit *= 2
    assert bit == subs
    sub_rounds = len(partners)
    bit = 1
    while bit < levels:
        partners.append({"level": flipped(level, bit)})
        bit *= 2
    assert bit == levels
    rounds = len(partners)

    barrier = pltpu.get_barrier_semaphore()
    for partner in partners:
        pl.semaphore_signal(barrier, inc=1, device_id=partner, device_id_type=MESH)

    @pl.when(has_up)
    def _():
        for partner in (above, {"sub": right}, {"sub": left}):
            pl.semaphore_signal(barrier, inc=1, device_id=partner, device_id_type=MESH)

    @pl.when(level > 0)
    def _():
        pl.semaphore_signal(barrier, inc=1, device_id=below, device_id_type=MESH)

    def remote(source, target, send, recv, device):
        return pltpu.make_async_remote_copy(
            src_ref=source,
            dst_ref=target,
            send_sem=send,
            recv_sem=recv,
            device_id=device,
            device_id_type=MESH,
        )

    def chunk_copies(source, target, send, recv, device):
        return [
            remote(source.at[c], target.at[c], send.at[c], recv.at[c], device)
            for c in range(chunks)
        ]

    give_copy = [
        remote(
            inverse_hbm.at[pl.ds(0, half), pl.ds(0, half)],
            top_corner,
            give_send.at[0],
            give_recv.at[0],
            below,
        ),
        remote(
            inverse_hbm.at[pl.ds(half, half)], top_rows, give_send.at[1], give_recv.at[1], below
        ),
    ]
    for c in range(chunks):
        give_copy.append(
            remote(
                rhs_hbm.at[:, pl.ds(c * LANES, LANES)],
                top_rhs.at[c],
                give_send.at[2 + c],
                give_recv.at[2 + c],
                below,
            )
        )
    next_copy = chunk_copies(next_out, next_in, next_send, next_recv, {"sub": right})
    up_copy = chunk_copies(own, up_in, up_send, up_recv, above)
    lift_copy = chunk_copies(own_in, solved, up_send, up_recv, above)
    down_copy = chunk_copies(solved, own_in, down_send, down_recv, below)
    side_copy = chunk_copies(own_in, beside_in, side_send, side_recv, {"sub": left})
    sums_copy = [
        remote(sums_out.at[r], sums_in.at[r], sums_send.at[r], sums_recv.at[r], partners[r])
        for r in range(rounds)
    ]

    def placed(slot):
        found = jnp.int32(0)
        for k in range(slots):
            found = jnp.where(rows_ref[k] == slot, k, found)
        return blocks[found]

    def spread_matrix(first):
        picked = [placed(first + d) for d in range(slots // 2)]
        ordered = jnp.concatenate(picked, axis=0)
        return product(left_operand(ordered), right_operand(inverse[...]))

    def squared(matrix):
        return left_operand(product(left_operand(matrix.T), right_operand(matrix)))

    def start_sums():
        for c in range(chunks):
            value = rhs[c]
            squares = (value * value).reshape(width // 8, 8, LANES)
            sums_out[0, :, pl.ds(c * LANES, LANES)] = jnp.sum(squares, axis=0)
        sums_copy[0].start()

    def next_sums(r):
        if r < rounds:
            sums_copy[r - 1].wait_recv()
            sums_out[r] = sums_out[r - 1] + sums_in[r - 1]
            sums_copy[r].start()

    def store(c, value):
        x_ref[:, pl.ds(c * LANES, LANES)] = value

    greetings = rounds + jnp.where(has_up, 3, 0) + jnp.where(level > 0, 1, 0)

    @pl.when(jnp.logical_and(is_top, jnp.logical_not(lent)))
    def _():
        inverse_load.wait()
        gram[...] = squared(inverse[...])
        for load in rhs_loads:
            load.wait()
        pl.semaphore_wait(barrier, greetings)
        start_sums()
        for c in range(chunks):
            up_copy[c].wait_recv()
            value = product(gram[...], right_operand(rhs[c] - up_in[c]))
            solved[c] = value
            down_copy[c].start()
            store(c, value)
            if c + 1 < sub_rounds:
                next_sums(c + 1)
        for r in range(chunks + 1, sub_rounds):
            next_sums(r)
        next_sums(sub_rounds)
        for c in range(chunks):
            down_copy[c].wait_send()

    @pl.when(jnp.logical_and(is_top, lent))
    def _():
        inverse_load.wait()
        pl.semaphore_wait(barrier, greetings)
        for copy in give_copy[:3]:
            copy.start()
        for load in rhs_loads:
            load.wait()
        start_sums()
        for n in range(3, 2 + chunks):
            if n == 3:
                give_copy[0].wait_send()
            give_copy[n - 2].wait_send()
            give_copy[n].start()
        for r in range(1, sub_rounds + 1):
            next_sums(r)
        for c in range(chunks):
            lift_copy[c].wait_recv()
            store(c, solved[c])
        for copy in give_copy[chunks:]:
            copy.wait_send()

    def make_next():
        matrix = spread_matrix(slots // 2)
        spread_next[...] = left_operand(matrix)

    def make_own():
        matrix = spread_matrix(0)
        spread_own[...] = left_operand(matrix)

    def make_turned():
        for matrix, turned in ((spread_own, turned_own), (spread_next, turned_next)):
            for piece in range(3):
                span = pl.ds(piece * width, width)
                turned[:, span] = matrix[:, span].T

    def send_next(operand, c):
        next_out[c] = product(spread_next[...], operand)
        next_copy[c].start()

    def finish(c):
        side_copy[c].wait_recv()
        value = base[c] - product(turned_next[...], right_operand(beside_in[c]))
        store(c, value)
        if levels > 2:

            @pl.when(level > 0)
            def _():
                solved[c] = value
                down_copy[c].start()

    @pl.when(has_up)
    def _():
        block_load.wait()
        inverse_load.wait()
        make_next()
        for load in rhs_loads:
            load.wait()
        pl.semaphore_wait(barrier, greetings)

    @pl.when(is_host)
    def _():
        if levels > 2:

            @pl.when(level > 0)
            def _():
                for c in range(chunks):
                    up_copy[c].wait_recv()

        def remaining(c):
            if levels == 2:
                return rhs[c]
            return rhs[c] - jnp.where(level > 0, up_in[c], 0.0)

        for c in range(chunks):
            next_out[c] = product(spread_next[...], right_operand(remaining(c)))
            if c < 2:
                next_copy[c].start()
        start_sums()
        make_own()
        for c in range(chunks):
            own[c] = product(spread_own[...], right_operand(remaining(c)))
        for c in range(2, chunks):
            next_copy[c - 2].wait_send()
            next_copy[c].start()
            if c == 2:
                gram[...] = squared(inverse[...])
                make_turned()
        for c in range(chunks):
            base[c] = product(gram[...], right_operand(remaining(c)))
        give_copy[0].wait_recv()
        give_copy[1].wait_recv()
        corner = jnp.concatenate([top_corner[...], jnp.zeros((half, half), jnp.float32)], axis=1)
        gram_top[...] = squared(jnp.concatenate([corner, top_rows[...]], axis=0))
        for c in range(chunks):
            next_copy[c].wait_recv()
            give_copy[2 + c].wait_recv()
            operand = right_operand(top_rhs[c] - (own[c] + next_in[c]))
            value = product(gram_top[...], operand)
            own_in[c] = value
            side_copy[c].start()
            lift_copy[c].start()
            base[c] = base[c] - product(turned_own[...], right_operand(value))
            if c + 1 < sub_rounds:
                next_sums(c + 1)
            if c > 0:
                finish(c - 1)
        for r in range(chunks + 1, sub_rounds):
            next_sums(r)
        next_sums(sub_rounds)
        finish(chunks - 1)
        for c in range(chunks):
            if c >= chunks - 2:
                next_copy[c].wait_send()
            lift_copy[c].wait_send()
            side_copy[c].wait_send()

    @pl.when(jnp.logical_and(has_up, jnp.logical_not(is_host)))
    def _():
        if levels > 2:

            @pl.when(level > 0)
            def _():
                for c in range(chunks):
                    up_copy[c].wait_recv()

        def remaining(c):
            if levels == 2:
                return rhs[c]
            return rhs[c] - jnp.where(level > 0, up_in[c], 0.0)

        make_own()
        for c in range(chunks):
            operand = right_operand(remaining(c))
            send_next(operand, c)
            own[c] = product(spread_own[...], operand)
        start_sums()
        for c in range(chunks):
            next_copy[c].wait_recv()
            own[c] = own[c] + next_in[c]
            up_copy[c].start()
        make_turned()
        gram[...] = squared(inverse[...])
        for c in range(chunks):
            base[c] = product(gram[...], right_operand(remaining(c)))
        for c in range(chunks):
            down_copy[c].wait_recv()
            side_copy[c].start()
            base[c] = base[c] - product(turned_own[...], right_operand(own_in[c]))
            if c + 1 < sub_rounds:
                next_sums(c + 1)
            if c > 0:
                finish(c - 1)
        for r in range(chunks + 1, sub_rounds):
            next_sums(r)
        next_sums(sub_rounds)
        finish(chunks - 1)
        for c in range(chunks):
            next_copy[c].wait_send()
            up_copy[c].wait_send()
            side_copy[c].wait_send()

    if levels > 2:

        @pl.when(jnp.logical_and(level > 0, has_up))
        def _():
            for c in range(chunks):
                down_copy[c].wait_send()

    for r in range(sub_rounds + 1, rounds):
        next_sums(r)
    sums_copy[rounds - 1].wait_recv()
    total = jnp.sum(sums_out[rounds - 1] + sums_in[rounds - 1], axis=0, keepdims=True)
    scale_ref[...] = jnp.sqrt(total / (levels * subs * width) + 1e-06)
    for r in range(rounds):
        sums_copy[r].wait_send()


def per_device(factor_inv, update_blocks, update_rows, right_side):
    levels = lax.axis_size("level")
    subs = lax.axis_size("sub")
    width = factor_inv.shape[-1]
    columns = right_side.shape[-1]
    slots, block_rows = update_blocks.shape[2:4]
    chunks = columns // LANES
    rounds = (levels * subs).bit_length() - 1
    piece = pltpu.VMEM((chunks, width, LANES), jnp.float32)
    wide = pltpu.VMEM((width, 3 * width), jnp.bfloat16)
    chunk_sem = pltpu.SemaphoreType.DMA((chunks,))
    round_sem = pltpu.SemaphoreType.DMA((rounds,))
    any_space = pl.BlockSpec(memory_space=pltpu.HBM)
    in_vmem = pl.BlockSpec(memory_space=pltpu.VMEM)
    value, col_scale = pl.pallas_call(
        functools.partial(kernel, levels, subs),
        out_shape=[
            jax.ShapeDtypeStruct((width, columns), jnp.float32),
            jax.ShapeDtypeStruct((1, columns), jnp.float32),
        ],
        in_specs=[
            pl.BlockSpec(memory_space=pltpu.SMEM),
            any_space,
            any_space,
            any_space,
        ],
        out_specs=[in_vmem, in_vmem],
        scratch_shapes=[
            pltpu.VMEM((width, width), jnp.float32),
            pltpu.VMEM((slots, block_rows, width), jnp.float32),
            piece,
        ]
        + [wide] * 6
        + [piece] * 8
        + [
            pltpu.VMEM((width // 2, width // 2), jnp.float32),
            pltpu.VMEM((width // 2, width), jnp.float32),
            piece,
            pltpu.VMEM((rounds, 8, columns), jnp.float32),
            pltpu.VMEM((rounds, 8, columns), jnp.float32),
        ]
        + [pltpu.SemaphoreType.DMA((2 + chunks,))] * 3
        + [chunk_sem] * 8
        + [round_sem] * 2,
        compiler_params=pltpu.CompilerParams(
            collective_id=0, has_side_effects=True, vmem_limit_bytes=60 * 1024 * 1024
        ),
        name="staircase",
    )(update_rows[0, 0], factor_inv[0, 0], update_blocks[0, 0], right_side[0, 0])
    return (value / col_scale)[None, None]


def solution(mesh):
    return jax.shard_map(
        per_device,
        mesh=mesh,
        in_specs=(
            P("level", "sub", None, None),
            P("level", "sub", None, None, None),
            P("level", "sub", None),
            P("level", "sub", None, None),
        ),
        out_specs=P("level", "sub", None, None),
        check_vma=False,
    )
```

```python
import functools

import jax
import jax.numpy as jnp
from jax import lax
from jax.experimental import pallas as pl
from jax.experimental.pallas import tpu as pltpu
from jax.sharding import PartitionSpec as P

LANES = 128
MESH = pl.DeviceIdType.MESH


def halves(value):
    high = value.astype(jnp.bfloat16)
    low = (value - high.astype(jnp.float32)).astype(jnp.bfloat16)
    return high, low


def left_operand(matrix):
    high, low = halves(matrix)
    return jnp.concatenate([high, low, high], axis=1)


def right_operand(values):
    high, low = halves(values)
    return jnp.concatenate([high, high, low], axis=0)


def product(left, right):
    return jnp.dot(left, right, preferred_element_type=jnp.float32)


def flipped(index, bit):
    return index + bit - 2 * bit * lax.rem(lax.div(index, bit), 2)


def kernel(
    levels,
    subs,
    rows_ref,
    inverse_hbm,
    blocks_hbm,
    rhs_hbm,
    x_ref,
    inverse,
    blocks,
    rhs,
    spread_own,
    spread_next,
    turned_own,
    turned_next,
    gram,
    gram_top,
    base,
    own,
    next_out,
    next_in,
    up_in,
    own_in,
    beside_in,
    solved,
    top_corner,
    top_rows,
    top_rhs,
    sums_out,
    sums_in,
    load_sem,
    give_send,
    give_recv,
    next_send,
    next_recv,
    up_send,
    up_recv,
    down_send,
    down_recv,
    side_send,
    side_recv,
    sums_send,
    sums_recv,
):
    level = lax.axis_index("level")
    sub = lax.axis_index("sub")
    chunks = rhs.shape[0]
    width = inverse.shape[0]
    half = width // 2
    slots = blocks.shape[0]
    right = lax.rem(sub + 1, subs)
    left = lax.rem(sub + subs - 1, subs)
    is_top = level == levels - 1
    lent = lax.rem(sub, 2) == 0
    is_host = jnp.logical_and(level == levels - 2, lent)
    has_up = level < levels - 1
    above = {"level": level + 1}
    below = {"level": level - 1}

    block_load = pltpu.make_async_copy(blocks_hbm, blocks, load_sem.at[0])
    inverse_load = pltpu.make_async_copy(inverse_hbm, inverse, load_sem.at[1])
    rhs_loads = [
        pltpu.make_async_copy(
            rhs_hbm.at[:, pl.ds(c * LANES, LANES)], rhs.at[c], load_sem.at[2 + c]
        )
        for c in range(chunks)
    ]

    @pl.when(has_up)
    def _():
        block_load.start()

    inverse_load.start()
    for load in rhs_loads:
        load.start()

    partners = []
    bit = 1
    while bit < subs:
        partners.append({"sub": flipped(sub, bit)})
        bit *= 2
    assert bit == subs
    sub_rounds = len(partners)
    bit = 1
    while bit < levels:
        partners.append({"level": flipped(level, bit)})
        bit *= 2
    assert bit == levels
    rounds = len(partners)

    barrier = pltpu.get_barrier_semaphore()
    for partner in partners:
        pl.semaphore_signal(barrier, inc=1, device_id=partner, device_id_type=MESH)

    @pl.when(has_up)
    def _():
        for partner in (above, {"sub": right}, {"sub": left}):
            pl.semaphore_signal(barrier, inc=1, device_id=partner, device_id_type=MESH)

    @pl.when(level > 0)
    def _():
        pl.semaphore_signal(barrier, inc=1, device_id=below, device_id_type=MESH)

    def remote(source, target, send, recv, device):
        return pltpu.make_async_remote_copy(
            src_ref=source,
            dst_ref=target,
            send_sem=send,
            recv_sem=recv,
            device_id=device,
            device_id_type=MESH,
        )

    def chunk_copies(source, target, send, recv, device):
        return [
            remote(source.at[c], target.at[c], send.at[c], recv.at[c], device)
            for c in range(chunks)
        ]

    give_copy = [
        remote(
            inverse_hbm.at[pl.ds(0, half), pl.ds(0, half)],
            top_corner,
            give_send.at[0],
            give_recv.at[0],
            below,
        ),
        remote(
            inverse_hbm.at[pl.ds(half, half)], top_rows, give_send.at[1], give_recv.at[1], below
        ),
    ]
    for c in range(chunks):
        give_copy.append(
            remote(
                rhs_hbm.at[:, pl.ds(c * LANES, LANES)],
                top_rhs.at[c],
                give_send.at[2 + c],
                give_recv.at[2 + c],
                below,
            )
        )
    next_copy = chunk_copies(next_out, next_in, next_send, next_recv, {"sub": right})
    up_copy = chunk_copies(own, up_in, up_send, up_recv, above)
    lift_copy = chunk_copies(own_in, solved, up_send, up_recv, above)
    down_copy = chunk_copies(solved, own_in, down_send, down_recv, below)
    side_copy = chunk_copies(own_in, beside_in, side_send, side_recv, {"sub": left})
    sums_copy = [
        remote(sums_out.at[r], sums_in.at[r], sums_send.at[r], sums_recv.at[r], partners[r])
        for r in range(rounds)
    ]

    def placed(slot):
        found = jnp.int32(0)
        for k in range(slots):
            found = jnp.where(rows_ref[k] == slot, k, found)
        return blocks[found]

    def spread_matrix(first):
        picked = [placed(first + d) for d in range(slots // 2)]
        ordered = jnp.concatenate(picked, axis=0)
        return product(left_operand(ordered), right_operand(inverse[...]))

    def squared(matrix):
        return left_operand(product(left_operand(matrix.T), right_operand(matrix)))

    def start_sums():
        for c in range(chunks):
            value = rhs[c]
            squares = (value * value).reshape(width // 8, 8, LANES)
            sums_out[0, :, pl.ds(c * LANES, LANES)] = jnp.sum(squares, axis=0)
        sums_copy[0].start()

    def next_sums(r):
        if r < rounds:
            sums_copy[r - 1].wait_recv()
            sums_out[r] = sums_out[r - 1] + sums_in[r - 1]
            sums_copy[r].start()

    def store(c, value):
        x_ref[:, pl.ds(c * LANES, LANES)] = value

    greetings = rounds + jnp.where(has_up, 3, 0) + jnp.where(level > 0, 1, 0)

    @pl.when(jnp.logical_and(is_top, jnp.logical_not(lent)))
    def _():
        inverse_load.wait()
        gram[...] = squared(inverse[...])
        for load in rhs_loads:
            load.wait()
        pl.semaphore_wait(barrier, greetings)
        start_sums()
        for c in range(chunks):
            up_copy[c].wait_recv()
            value = product(gram[...], right_operand(rhs[c] - up_in[c]))
            solved[c] = value
            down_copy[c].start()
            store(c, value)
            if c + 1 < sub_rounds:
                next_sums(c + 1)
        for r in range(chunks + 1, sub_rounds):
            next_sums(r)
        next_sums(sub_rounds)
        for c in range(chunks):
            down_copy[c].wait_send()

    @pl.when(jnp.logical_and(is_top, lent))
    def _():
        inverse_load.wait()
        pl.semaphore_wait(barrier, greetings)
        for copy in give_copy[:3]:
            copy.start()
        for load in rhs_loads:
            load.wait()
        start_sums()
        for n in range(3, 2 + chunks):
            if n == 3:
                give_copy[0].wait_send()
            give_copy[n - 2].wait_send()
            give_copy[n].start()
        for r in range(1, sub_rounds + 1):
            next_sums(r)
        for c in range(chunks):
            lift_copy[c].wait_recv()
            store(c, solved[c])
        for copy in give_copy[chunks:]:
            copy.wait_send()

    def make_next():
        matrix = spread_matrix(slots // 2)
        spread_next[...] = left_operand(matrix)

    def make_own():
        matrix = spread_matrix(0)
        spread_own[...] = left_operand(matrix)

    def make_turned():
        for matrix, turned in ((spread_own, turned_own), (spread_next, turned_next)):
            for piece in range(3):
                span = pl.ds(piece * width, width)
                turned[:, span] = matrix[:, span].T

    def send_next(operand, c):
        next_out[c] = product(spread_next[...], operand)
        next_copy[c].start()

    def finish(c):
        side_copy[c].wait_recv()
        value = base[c] - product(turned_next[...], right_operand(beside_in[c]))
        store(c, value)
        if levels > 2:

            @pl.when(level > 0)
            def _():
                solved[c] = value
                down_copy[c].start()

    @pl.when(has_up)
    def _():
        block_load.wait()
        inverse_load.wait()
        make_next()
        for load in rhs_loads:
            load.wait()
        pl.semaphore_wait(barrier, greetings)

    @pl.when(is_host)
    def _():
        if levels > 2:

            @pl.when(level > 0)
            def _():
                for c in range(chunks):
                    up_copy[c].wait_recv()

        def remaining(c):
            if levels == 2:
                return rhs[c]
            return rhs[c] - jnp.where(level > 0, up_in[c], 0.0)

        for c in range(chunks):
            next_out[c] = product(spread_next[...], right_operand(remaining(c)))
            if c < 2:
                next_copy[c].start()
        start_sums()
        make_own()
        for c in range(chunks):
            own[c] = product(spread_own[...], right_operand(remaining(c)))
        for c in range(2, chunks):
            next_copy[c - 2].wait_send()
            next_copy[c].start()
            if c == 2:
                gram[...] = squared(inverse[...])
                make_turned()
        for c in range(chunks):
            base[c] = product(gram[...], right_operand(remaining(c)))
        give_copy[0].wait_recv()
        give_copy[1].wait_recv()
        corner = jnp.concatenate([top_corner[...], jnp.zeros((half, half), jnp.float32)], axis=1)
        gram_top[...] = squared(jnp.concatenate([corner, top_rows[...]], axis=0))
        for c in range(chunks):
            next_copy[c].wait_recv()
            give_copy[2 + c].wait_recv()
            operand = right_operand(top_rhs[c] - (own[c] + next_in[c]))
            value = product(gram_top[...], operand)
            own_in[c] = value
            side_copy[c].start()
            lift_copy[c].start()
            base[c] = base[c] - product(turned_own[...], right_operand(value))
            if c + 1 < sub_rounds:
                next_sums(c + 1)
            if c > 0:
                finish(c - 1)
        for r in range(chunks + 1, sub_rounds):
            next_sums(r)
        next_sums(sub_rounds)
        finish(chunks - 1)
        for c in range(chunks):
            if c >= chunks - 2:
                next_copy[c].wait_send()
            lift_copy[c].wait_send()
            side_copy[c].wait_send()

    @pl.when(jnp.logical_and(has_up, jnp.logical_not(is_host)))
    def _():
        if levels > 2:

            @pl.when(level > 0)
            def _():
                for c in range(chunks):
                    up_copy[c].wait_recv()

        def remaining(c):
            if levels == 2:
                return rhs[c]
            return rhs[c] - jnp.where(level > 0, up_in[c], 0.0)

        make_own()
        for c in range(chunks):
            operand = right_operand(remaining(c))
            send_next(operand, c)
            own[c] = product(spread_own[...], operand)
        start_sums()
        for c in range(chunks):
            next_copy[c].wait_recv()
            own[c] = own[c] + next_in[c]
            up_copy[c].start()
        make_turned()
        gram[...] = squared(inverse[...])
        for c in range(chunks):
            base[c] = product(gram[...], right_operand(remaining(c)))
        for c in range(chunks):
            down_copy[c].wait_recv()
            side_copy[c].start()
            base[c] = base[c] - product(turned_own[...], right_operand(own_in[c]))
            if c + 1 < sub_rounds:
                next_sums(c + 1)
            if c > 0:
                finish(c - 1)
        for r in range(chunks + 1, sub_rounds):
            next_sums(r)
        next_sums(sub_rounds)
        finish(chunks - 1)
        for c in range(chunks):
            next_copy[c].wait_send()
            up_copy[c].wait_send()
            side_copy[c].wait_send()

    if levels > 2:

        @pl.when(jnp.logical_and(level > 0, has_up))
        def _():
            for c in range(chunks):
                down_copy[c].wait_send()

    for r in range(sub_rounds + 1, rounds):
        next_sums(r)
    sums_copy[rounds - 1].wait_recv()
    total = jnp.sum(sums_out[rounds - 1] + sums_in[rounds - 1], axis=0, keepdims=True)
    x_ref[...] = x_ref[...] / jnp.sqrt(total / (levels * subs * width) + 1e-06)
    for r in range(rounds):
        sums_copy[r].wait_send()


def per_device(factor_inv, update_blocks, update_rows, right_side):
    levels = lax.axis_size("level")
    subs = lax.axis_size("sub")
    width = factor_inv.shape[-1]
    columns = right_side.shape[-1]
    slots, block_rows = update_blocks.shape[2:4]
    chunks = columns // LANES
    rounds = (levels * subs).bit_length() - 1
    piece = pltpu.VMEM((chunks, width, LANES), jnp.float32)
    wide = pltpu.VMEM((width, 3 * width), jnp.bfloat16)
    chunk_sem = pltpu.SemaphoreType.DMA((chunks,))
    round_sem = pltpu.SemaphoreType.DMA((rounds,))
    any_space = pl.BlockSpec(memory_space=pltpu.HBM)
    in_vmem = pl.BlockSpec(memory_space=pltpu.VMEM)
    value = pl.pallas_call(
        functools.partial(kernel, levels, subs),
        out_shape=jax.ShapeDtypeStruct((width, columns), jnp.float32),
        in_specs=[
            pl.BlockSpec(memory_space=pltpu.SMEM),
            any_space,
            any_space,
            any_space,
        ],
        out_specs=in_vmem,
        scratch_shapes=[
            pltpu.VMEM((width, width), jnp.float32),
            pltpu.VMEM((slots, block_rows, width), jnp.float32),
            piece,
        ]
        + [wide] * 6
        + [piece] * 8
        + [
            pltpu.VMEM((width // 2, width // 2), jnp.float32),
            pltpu.VMEM((width // 2, width), jnp.float32),
            piece,
            pltpu.VMEM((rounds, 8, columns), jnp.float32),
            pltpu.VMEM((rounds, 8, columns), jnp.float32),
        ]
        + [pltpu.SemaphoreType.DMA((2 + chunks,))] * 3
        + [chunk_sem] * 8
        + [round_sem] * 2,
        compiler_params=pltpu.CompilerParams(
            collective_id=0, has_side_effects=True, vmem_limit_bytes=60 * 1024 * 1024
        ),
        name="staircase",
    )(update_rows[0, 0], factor_inv[0, 0], update_blocks[0, 0], right_side[0, 0])
    return value[None, None]


def solution(mesh):
    return jax.shard_map(
        per_device,
        mesh=mesh,
        in_specs=(
            P("level", "sub", None, None),
            P("level", "sub", None, None, None),
            P("level", "sub", None),
            P("level", "sub", None, None),
        ),
        out_specs=P("level", "sub", None, None),
        check_vma=False,
    )
```
